32 devices in a mesh: groups: 2 (over y), section: 4 (over x, core), lat: 4 (over z).
Axes of the slice: x: 2, y: 2, z: 4, core: 2. Of those that a mesh axis runs over, the one named last changes fastest.
Arguments:
- member_slabs: float32 [8, 16, 64, 768], P(('groups', 'section'), 'lat'), parts along dimension 0, may hold values from -6 to 6
- member_codes: int32 [2, 8], P(None, 'groups'), parts along dimension 1, may hold values from 0 to 31
- member_table: float32 [32, 768], replicated, may hold values from -4 to 4
- land_sea: int32 [16, 64], P('lat'), may hold values 0 or 1
- land_embed: float32 [4, 768], P('section'), may hold values from -4 to 4
- attention_gain: float32 [4, 768], P('section'), may hold values from 0.25 to 1.75
- project_in: bfloat16 [4, 768, 2304], P('section'), may hold values from -0.21875 to 0.21875
- logit_scale: float32 [4, 12], P('section'), may hold values from 3 to 25
- position_kernel: float32 [4, 5, 3, 768], P('section'), may hold values from -1.5 to 1.5
- project_out: bfloat16 [4, 768, 768], P('section'), may hold values from -0.21875 to 0.21875
- feed_gain: float32 [4, 768], P('section'), may hold values from 0.25 to 1.75
- expand_weight: bfloat16 [4, 768, 2048], P('section'), may hold values from -0.21875 to 0.21875
- reduce_weight: bfloat16 [4, 2048, 768], P('section'), may hold values from -0.125 to 0.125
- window_offset: int32 [4], P('section'), may hold values from 1 to 31
Outputs:
- updated_slabs: float32 [8, 16, 64, 768], P(('groups', 'section'), 'lat'), parts along dimension 0
The draws below stay inside these ranges and needn't reach their ends.
There are 2 independent parts, one for each index of `groups`. The reference program is written for one: setup_inputs(seed, part) draws one part's arguments, and reference() takes and returns one part's arrays. A program takes and returns all parts, laid end to end along the dimension named above; an argument that names none is the same for every part. Nothing has to cross between parts.
Inputs may be any that keep to these rules, and one draw needn't show every extreme that they name: member_codes[t, m] names the perturbation embedding of member m at tick t. `land_sea`: 1 marks land.
All inputs are finite; a program needn't handle non-finite values. No bound on the sum of `land_sea` on one device may be relied on, other than what follows from the above.
Results may differ from the reference program's by a relative error of at most 0.0085.
Values may be sent and summed in bfloat16 or wider, within the bound.
A program may use at most 128 MiB of HBM per device.

```python
import math
import jax
import jax.numpy as jnp
from jax import lax

D = 768
HEADS = 12
FF = 2048
WIN_LAT = 4
WIN_LON = 32
LONS = 64
TICKS = 2
TABLE = 32
LATS = 16
LAYERS = 4
MEMBERS = 4
N_SECTION = 4


def with_ends(result, rng, smallest, top_value):
    longest = result.shape.index(max(result.shape))
    spots = []
    for shift in (0, 1):
        where = [jax.random.randint(jax.random.fold_in(rng, axis), (), 0, length) for axis, length in enumerate(result.shape)]
        where[longest] = (where[longest] + shift) % result.shape[longest]
        spots.append(tuple(where))
    return result.at[spots[0]].set(smallest).at[spots[1]].set(top_value)


def levels(key, shape, cuts, least, largest):
    factor_of, own = 1.0, jax.random.fold_in(key, 6)
    for dim, parts in cuts:
        draws = jnp.exp(jax.random.uniform(jax.random.fold_in(own, dim), (parts,), jnp.float32, least / len(cuts), largest / len(cuts)))
        factor_of = factor_of * jnp.repeat(draws, shape[dim] // parts).reshape([-1 if axis == dim else 1 for axis in range(len(shape))])
    return factor_of


def normal_values(key, extent, spread, limit, cuts=(), kind=jnp.bfloat16):
    loudness = levels(key, extent, cuts, -0.22, 0.18) if cuts else 1.0
    entries = jax.random.normal(key, extent, jnp.float32) * spread * loudness
    return jnp.minimum(jnp.maximum(entries, -limit), limit).astype(kind)


def setup_inputs(seed: int = 0, part: int = 0) -> dict:
    key_list = jax.random.split(jax.random.key(seed), 15)
    part_splits = jax.random.split(jax.random.fold_in(key_list[14], part), 15)
    member_slabs = normal_values(part_splits[0], (MEMBERS, LATS, LONS, D), 1.0, 6.0, ((0, 4), (1, 4)), jnp.float32)
    member_codes = with_ends(jax.random.randint(part_splits[1], (TICKS, MEMBERS), 0, TABLE), jax.random.fold_in(part_splits[1], 1), 0, TABLE - 1).astype(jnp.int32)
    member_table = normal_values(key_list[2], (TABLE, D), 0.5, 4.0, (), jnp.float32)
    land_sea = with_ends((jax.random.randint(key_list[3], (LATS, LONS), 0, 10) < 3).astype(jnp.int32), jax.random.fold_in(key_list[3], 1), 0, 1)
    land_embed = normal_values(key_list[4], (LAYERS, D), 0.5, 4.0, ((0, 4),), jnp.float32)
    attention_gain = jnp.clip(1.0 + 0.15 * jax.random.normal(key_list[5], (LAYERS, D), jnp.float32), 0.25, 1.75)
    project_in = normal_values(key_list[6], (LAYERS, D, 3 * D), D ** -0.5, 0.21875, ((0, 4),))
    logit_scale = jnp.clip(jnp.exp(math.log(25.0) - 2.1202635 * jax.random.uniform(key_list[7], (LAYERS, HEADS), jnp.float32) ** levels(key_list[7], (LAYERS, HEADS), ((0, 4),), -0.2, 0.2)), 3.0, 25.0)
    position_kernel = normal_values(key_list[8], (LAYERS, WIN_LAT + 1, 3, D), (3 * (WIN_LAT + 1)) ** -0.5, 1.5, ((0, 4),), jnp.float32)
    project_out = normal_values(key_list[9], (LAYERS, D, D), D ** -0.5, 0.21875, ((0, 4),))
    feed_gain = jnp.clip(1.0 + 0.15 * jax.random.normal(key_list[10], (LAYERS, D), jnp.float32), 0.25, 1.75)
    expand_weight = normal_values(key_list[11], (LAYERS, D, FF), D ** -0.5, 0.21875, ((0, 4),))
    reduce_weight = normal_values(key_list[12], (LAYERS, FF, D), FF ** -0.5, 0.125, ((0, 4),))
    window_offset = with_ends(jax.random.randint(key_list[13], (LAYERS,), 1, WIN_LON), jax.random.fold_in(key_list[13], 1), 1, WIN_LON - 1).astype(jnp.int32)
    return {"member_slabs": member_slabs, "member_codes": member_codes, "member_table": member_table, "land_sea": land_sea, "land_embed": land_embed, "attention_gain": attention_gain, "project_in": project_in, "logit_scale": logit_scale, "position_kernel": position_kernel, "project_out": project_out, "feed_gain": feed_gain, "expand_weight": expand_weight, "reduce_weight": reduce_weight, "window_offset": window_offset}


EPSILON = 1e-06

def norm_scale(values, gain_row):
    mean_square = lax.optimization_barrier(jnp.mean(values * values, axis=-1, keepdims=True))
    return values * lax.rsqrt(mean_square + EPSILON) * gain_row

def head_unit(values):
    shaped = values.reshape(values.shape[:-1] + (HEADS, values.shape[-1] // HEADS))
    square_sum = lax.optimization_barrier(jnp.sum(shaped * shaped, axis=-1, keepdims=True))
    return (shaped * lax.rsqrt(square_sum + EPSILON)).astype(jnp.bfloat16)

def position_term(value_rows, kernel, band_rows):
    totals = jnp.zeros((band_rows,) + value_rows.shape[1:], jnp.float32)
    for lat_step in range(kernel.shape[0]):
        strip_rows = value_rows[lat_step:lat_step + band_rows]
        for lon_step in range(kernel.shape[1]):
            totals = totals + kernel[lat_step, lon_step] * jnp.roll(strip_rows, 1 - lon_step, axis=1)
    return totals

def window_attend(query_tiles, key_tiles, value_tiles, row_valid, head_scale):
    row_count, lon_count, head_count, head_width = query_tiles.shape
    tile_rows = row_count // WIN_LAT
    tile_cols = lon_count // WIN_LON

    def to_tiles(block_in):
        shaped = block_in.reshape(tile_rows, WIN_LAT, tile_cols, WIN_LON, head_count, head_width)
        shaped = shaped.transpose(0, 2, 4, 1, 3, 5)
        return shaped.reshape(tile_rows, tile_cols, head_count, WIN_LAT * WIN_LON, head_width)
    query_set = to_tiles(query_tiles).astype(jnp.float32)
    key_set = to_tiles(key_tiles).astype(jnp.float32)
    value_set = to_tiles(value_tiles).astype(jnp.float32)
    scores = jnp.einsum('abhqd,abhkd->abhqk', query_set, key_set) * head_scale.reshape(1, 1, head_count, 1, 1)
    key_keep = jnp.broadcast_to(row_valid.reshape(tile_rows, 1, 1, 1, WIN_LAT, 1), (tile_rows, 1, 1, 1, WIN_LAT, WIN_LON))
    key_keep = key_keep.reshape(tile_rows, 1, 1, 1, WIN_LAT * WIN_LON).astype(jnp.float32)
    raised = jnp.exp(scores) * key_keep
    weights = (raised / lax.optimization_barrier(jnp.sum(raised, axis=-1, keepdims=True))).astype(jnp.bfloat16)
    weights = lax.optimization_barrier(weights).astype(jnp.float32)
    attended = jnp.einsum('abhqk,abhkd->abhqd', weights, value_set)
    regrid = attended.reshape(tile_rows, tile_cols, head_count, WIN_LAT, WIN_LON, head_width).transpose(0, 3, 1, 4, 2, 5)
    return regrid.reshape(row_count, lon_count, head_count * head_width)

def apply_layer(current, perturb, land_sea, layer_index, land_embed, attention_gain, project_in, logit_scale, position_kernel, project_out, feed_gain, expand_weight, reduce_weight, window_offset):
    band_rows, lon_cells, features = current.shape
    halo_rows = WIN_LAT // 2
    head_width = features // HEADS
    stream = current + perturb + land_sea.astype(jnp.float32)[:, :, None] * land_embed[layer_index]
    normed = norm_scale(stream, attention_gain[layer_index]).astype(jnp.bfloat16).reshape(-1, features)
    queries = jnp.dot(normed, project_in[layer_index][:, :features], preferred_element_type=jnp.float32)
    key_value = jnp.dot(normed, project_in[layer_index][:, features:], preferred_element_type=jnp.float32)
    query_unit = head_unit(queries).reshape(band_rows, lon_cells, HEADS, head_width)
    key_unit = head_unit(key_value[:, :features]).reshape(band_rows, lon_cells, HEADS, head_width)
    value_half = key_value[:, features:].astype(jnp.bfloat16).reshape(band_rows, lon_cells, features)
    value_float = lax.optimization_barrier(value_half).astype(jnp.float32)
    value_padded = jnp.pad(value_float, ((halo_rows, halo_rows), (0, 0), (0, 0)))
    position = position_term(value_padded, position_kernel[layer_index], band_rows)
    value_heads = value_half.reshape(band_rows, lon_cells, HEADS, head_width)
    if layer_index % 2 == 1:
        offset = window_offset[layer_index]
        row_pad = ((halo_rows, halo_rows), (0, 0), (0, 0), (0, 0))

        def prepare(block_in):
            return jnp.roll(jnp.pad(block_in, row_pad), -offset, axis=1)
        row_valid = jnp.pad(jnp.ones((band_rows,), bool), (halo_rows, halo_rows))
        attended = window_attend(prepare(query_unit), prepare(key_unit), prepare(value_heads), row_valid, logit_scale[layer_index])
        attended = jnp.roll(attended, offset, axis=1)[halo_rows:halo_rows + band_rows]
    else:
        attended = window_attend(query_unit, key_unit, value_heads, jnp.ones((band_rows,), bool), logit_scale[layer_index])
    blended = (attended + position).astype(jnp.bfloat16).reshape(-1, features)
    after_mix = stream + jnp.dot(blended, project_out[layer_index], preferred_element_type=jnp.float32).reshape(stream.shape)
    normed_mix = norm_scale(after_mix, feed_gain[layer_index]).astype(jnp.bfloat16).reshape(-1, features)
    hidden = jax.nn.gelu(jnp.dot(normed_mix, expand_weight[layer_index], preferred_element_type=jnp.float32), approximate=False).astype(jnp.bfloat16)
    return after_mix + jnp.dot(hidden, reduce_weight[layer_index], preferred_element_type=jnp.float32).reshape(stream.shape)

def reference(member_slabs, member_codes, member_table, land_sea, land_embed, attention_gain, project_in, logit_scale, position_kernel, project_out, feed_gain, expand_weight, reduce_weight, window_offset):
    current = member_slabs
    for tick_index in range(TICKS):
        updated = []
        for section_index in range(N_SECTION):
            member = (section_index - tick_index) % N_SECTION
            perturb = member_table[member_codes[tick_index, member]]
            updated.append(apply_layer(current[section_index], perturb, land_sea, section_index, land_embed, attention_gain, project_in, logit_scale, position_kernel, project_out, feed_gain, expand_weight, reduce_weight, window_offset))
        current = jnp.stack(updated)
        if tick_index + 1 < TICKS:
            current = jnp.roll(current, 1, axis=0)
    return current
```

```python
import functools
import math

import jax
import jax.numpy as jnp
from jax import lax
from jax.experimental import pallas as pl
from jax.experimental.pallas import tpu as pltpu
from jax.sharding import PartitionSpec as P

WIN_LAT = 4
WIN_LON = 32
TICKS = 2
EPSILON = 1e-06

F32 = jnp.float32
BF16 = jnp.bfloat16
LANES = 128
COLS = 256
MESH = pl.DeviceIdType.MESH


def norm_scale(values, gain_row):
    mean_square = jnp.mean(values * values, axis=-1, keepdims=True)
    return values * lax.rsqrt(mean_square + EPSILON) * gain_row


def dot(left, right):
    return jnp.dot(left, right, preferred_element_type=F32)


def head_unit(values, head_width):
    groups = []
    for start in range(0, values.shape[1], LANES):
        part = values[:, start : start + LANES]
        lane = lax.broadcasted_iota(jnp.int32, part.shape, 1)
        square = part * part
        factor = None
        for low in range(0, LANES, head_width):
            inside = (lane >= low) & (lane < low + head_width)
            total = jnp.sum(jnp.where(inside, square, 0.0), axis=-1, keepdims=True)
            scale = lax.rsqrt(total + EPSILON)
            factor = scale if factor is None else jnp.where(inside, scale, factor)
        groups.append((part * factor).astype(BF16))
    return jnp.concatenate(groups, axis=1)


def split_index(index, length, count):
    whole = jnp.zeros_like(index)
    for step in range(1, count):
        whole = whole + (index >= step * length).astype(jnp.int32)
    return whole, index - whole * length


def kernel(
    sizes,
    codes,
    offsets,
    head_scale,
    slab,
    table,
    land,
    land_embed,
    attention_gain,
    feed_gain,
    position_kernel,
    in_hbm,
    out_hbm,
    up_hbm,
    down_hbm,
    result,
    w_in,
    w_out,
    w_up,
    w_down,
    stream,
    mixed,
    normed,
    halo,
    queries,
    keys,
    values,
    blended,
    normed_mix,
    hidden,
    window,
    ring_out,
    ring_in,
    weight_sem,
    halo_send,
    halo_recv,
    ring_send,
    ring_recv,
):
    section_count, band_count, lon_cells, head_width = sizes
    tokens, features = slab.shape
    band_rows = tokens // lon_cells
    half = tokens // 2
    per_group = LANES // head_width
    section = lax.axis_index("section")
    band = lax.axis_index("lat")
    following = lax.rem(section + 1, section_count)
    preceding = lax.rem(section + section_count - 1, section_count)
    has_low = band > 0
    has_high = band < band_count - 1
    shifted = lax.rem(section, 2)

    barrier = pltpu.get_barrier_semaphore()
    pl.semaphore_signal(barrier, inc=1, device_id={"section": following}, device_id_type=MESH)
    pl.semaphore_signal(barrier, inc=1, device_id={"section": preceding}, device_id_type=MESH)

    @pl.when(has_low)
    def _():
        pl.semaphore_signal(barrier, inc=1, device_id={"lat": band - 1}, device_id_type=MESH)

    @pl.when(has_high)
    def _():
        pl.semaphore_signal(barrier, inc=1, device_id={"lat": band + 1}, device_id_type=MESH)

    loads = [
        pltpu.make_async_copy(source, target, weight_sem.at[index])
        for index, (source, target) in enumerate(
            ((in_hbm, w_in), (out_hbm, w_out), (up_hbm, w_up), (down_hbm, w_down))
        )
    ]
    for load in loads:
        load.start()

    offset = offsets[0] * shifted
    key_starts = [half * (1 - shifted), half + half * shifted]
    for side in range(2):
        shape = (half, tokens)
        first_row = band * band_rows - band_rows // 2 + (
            (1 - shifted) * (band_rows // 2) if side == 0 else (1 + shifted) * (band_rows // 2)
        )
        _, query_lon = split_index(lax.broadcasted_iota(jnp.int32, shape, 0), lon_cells, band_rows)
        key_row, key_lon = split_index(lax.broadcasted_iota(jnp.int32, shape, 1), lon_cells, band_rows)
        tiles = []
        for lon in (query_lon, key_lon):
            moved = lon - offset
            moved = jnp.where(moved < 0, moved + lon_cells, moved)
            tiles.append(split_index(moved, WIN_LON, lon_cells // WIN_LON)[0])
        row = key_row + first_row
        inside = (tiles[0] == tiles[1]) & (row >= 0) & (row < band_rows * band_count)
        window[side] = jnp.where(inside, 1.0, 0.0)

    def project(source, target_rows, with_queries):
        def step(index, carry):
            start = pl.multiple_of(index * COLS, COLS)
            columns = pl.ds(start, COLS)
            rows = source[...]
            if with_queries:
                queries[:, columns] = head_unit(dot(rows, w_in[:, columns]), head_width)
            key = head_unit(
                dot(rows, w_in[:, pl.ds(pl.multiple_of(features + start, COLS), COLS)]), head_width
            )
            value = dot(
                rows, w_in[:, pl.ds(pl.multiple_of(2 * features + start, COLS), COLS)]
            ).astype(BF16)
            done = 0
            for first, count in target_rows:
                keys[first : first + count, columns] = key[done : done + count]
                values[first : first + count, columns] = value[done : done + count]
                done += count
            return carry

        lax.fori_loop(0, features // COLS, step, 0)

    def attend(index, carry):
        columns = pl.ds(pl.multiple_of(index * LANES, LANES), LANES)
        lane = lax.broadcasted_iota(jnp.int32, (1, LANES), 1)
        own = [
            jnp.where((lane >= low) & (lane < low + head_width), 1.0, 0.0).astype(BF16)
            for low in range(0, LANES, head_width)
        ]
        taps = [
            [position_kernel[lat, pl.ds(lon, 1), columns] for lon in range(3)]
            for lat in range(WIN_LAT + 1)
        ]
        for side in range(2):
            spots = []
            for row in range(side * band_rows // 2, (side + 1) * band_rows // 2):
                strips = [
                    values[(row + lat) * lon_cells : (row + lat + 1) * lon_cells, columns].astype(F32)
                    for lat in range(WIN_LAT + 1)
                ]
                parts = []
                for lon in range(3):
                    part = taps[0][lon] * strips[0]
                    for lat in range(1, WIN_LAT + 1):
                        part = part + taps[lat][lon] * strips[lat]
                    parts.append(part)
                spots.append(
                    parts[1]
                    + pltpu.roll(parts[0], 1, 0)
                    + pltpu.roll(parts[2], lon_cells - 1, 0)
                )
            total = jnp.concatenate(spots, axis=0)
            near = pl.ds(pl.multiple_of(key_starts[side], half), tokens)
            key = keys[near, columns]
            value = values[near, columns]
            query = queries[side * half : (side + 1) * half, columns]
            for head in range(per_group):
                scores = lax.dot_general(
                    query * own[head], key, (((1,), (1,)), ((), ())), preferred_element_type=F32
                )
                raised = jnp.exp(scores * head_scale[index * per_group + head]) * window[side]
                inverse = 1.0 / jnp.sum(raised, axis=-1, keepdims=True)
                total = total + dot((raised * inverse).astype(BF16), value * own[head])
            blended[side * half : (side + 1) * half, columns] = total.astype(BF16)
        return carry

    def expand(index, carry):
        columns = pl.ds(pl.multiple_of(index * COLS, COLS), COLS)
        wide = dot(normed_mix[...], w_up[:, columns])
        hidden[:, columns] = (wide * 0.5 * (1.0 + lax.erf(wide * math.sqrt(0.5)))).astype(BF16)
        return carry

    def halo_copies(tick):
        up = pltpu.make_async_remote_copy(
            src_ref=normed.at[tick, pl.ds(half, half)],
            dst_ref=halo.at[tick, pl.ds(0, half)],
            send_sem=halo_send.at[tick, 0],
            recv_sem=halo_recv.at[tick, 0],
            device_id={"lat": jnp.minimum(band + 1, band_count - 1)},
            device_id_type=MESH,
        )
        down = pltpu.make_async_remote_copy(
            src_ref=normed.at[tick, pl.ds(0, half)],
            dst_ref=halo.at[tick, pl.ds(half, half)],
            send_sem=halo_send.at[tick, 1],
            recv_sem=halo_recv.at[tick, 1],
            device_id={"lat": jnp.maximum(band - 1, 0)},
            device_id_type=MESH,
        )
        return up, down

    def ring_copy(tick, part):
        columns = pl.ds(part * COLS, COLS)
        return pltpu.make_async_remote_copy(
            src_ref=ring_out.at[tick, :, columns],
            dst_ref=ring_in.at[tick, :, columns],
            send_sem=ring_send.at[tick, part],
            recv_sem=ring_recv.at[tick, part],
            device_id={"section": following},
            device_id_type=MESH,
        )

    parts = features // COLS
    for tick in range(TICKS):
        if tick:
            for part in range(parts):
                ring_copy(tick - 1, part).wait()
        member = lax.rem(section - tick + section_count * TICKS, section_count)
        code = codes[tick, member]
        table_row = lax.broadcasted_iota(jnp.int32, table.shape, 0)
        perturb = jnp.sum(jnp.where(table_row == code, table[...], 0.0), axis=0, keepdims=True)

        def enter(index, carry):
            rows = pl.ds(pl.multiple_of(index * lon_cells, lon_cells), lon_cells)
            current = slab[rows, :] if tick == 0 else ring_in[tick - 1, rows, :].astype(F32)
            current = current + perturb + land[rows, :] * land_embed[...]
            stream[rows, :] = current
            normed[tick, rows, :] = norm_scale(current, attention_gain[...]).astype(BF16)
            return carry

        lax.fori_loop(0, band_rows, enter, 0)

        if tick == 0:
            ends = (band == 0).astype(jnp.int32) + (band == band_count - 1).astype(jnp.int32)
            pl.semaphore_wait(barrier, 4 - ends)

        up, down = halo_copies(tick)

        @pl.when(has_high)
        def _():
            up.start()

        @pl.when(has_low)
        def _():
            down.start()

        @pl.when(jnp.logical_not(has_low))
        def _():
            halo[tick, 0:half, :] = jnp.zeros((half, features), BF16)

        @pl.when(jnp.logical_not(has_high))
        def _():
            halo[tick, half:tokens, :] = jnp.zeros((half, features), BF16)

        if tick == 0:
            loads[0].wait()
        project(normed.at[tick], ((half, tokens),), True)

        @pl.when(has_high)
        def _():
            up.wait_send()
            down.wait_recv()

        @pl.when(has_low)
        def _():
            down.wait_send()
            up.wait_recv()

        project(halo.at[tick], ((0, half), (half + tokens, half)), False)
        lax.fori_loop(0, features // LANES, attend, 0)

        if tick == 0:
            loads[1].wait()
        for part in range(parts):
            columns = slice(part * COLS, (part + 1) * COLS)
            mixed[:, columns] = stream[:, columns] + dot(blended[...], w_out[:, columns])

        def middle(index, carry):
            rows = pl.ds(pl.multiple_of(index * lon_cells, lon_cells), lon_cells)
            normed_mix[rows, :] = norm_scale(mixed[rows, :], feed_gain[...]).astype(BF16)
            return carry

        lax.fori_loop(0, band_rows, middle, 0)
        if tick == 0:
            loads[2].wait()
        lax.fori_loop(0, w_up.shape[1] // COLS, expand, 0)
        if tick == 0:
            loads[3].wait()
        for part in range(parts):
            columns = slice(part * COLS, (part + 1) * COLS)
            finished = mixed[:, columns] + dot(hidden[...], w_down[:, columns])
            if tick + 1 < TICKS:
                ring_out[tick, :, columns] = finished.astype(BF16)
                ring_copy(tick, part).start()
            else:
                result[:, columns] = finished


def solution(mesh):
    section_count = mesh.shape["section"]
    band_count = mesh.shape["lat"]

    def body(
        member_slabs,
        member_codes,
        member_table,
        land_sea,
        land_embed,
        attention_gain,
        project_in,
        logit_scale,
        position_kernel,
        project_out,
        feed_gain,
        expand_weight,
        reduce_weight,
        window_offset,
    ):
        _, band_rows, lon_cells, features = member_slabs.shape
        assert band_rows == WIN_LAT
        tokens = band_rows * lon_cells
        hidden_width = expand_weight.shape[2]
        head_width = features // logit_scale.shape[1]
        parts = features // COLS
        links = max(TICKS - 1, 1)
        smem = pl.BlockSpec(memory_space=pltpu.SMEM)
        vmem = pl.BlockSpec(memory_space=pltpu.VMEM)
        hbm = pl.BlockSpec(memory_space=pl.ANY)
        updated = pl.pallas_call(
            functools.partial(kernel, (section_count, band_count, lon_cells, head_width)),
            out_shape=jax.ShapeDtypeStruct((tokens, features), F32),
            in_specs=[smem] * 3 + [vmem] * 7 + [hbm] * 4,
            out_specs=vmem,
            scratch_shapes=[
                pltpu.VMEM((features, 3 * features), BF16),
                pltpu.VMEM((features, features), BF16),
                pltpu.VMEM((features, hidden_width), BF16),
                pltpu.VMEM((hidden_width, features), BF16),
                pltpu.VMEM((tokens, features), F32),
                pltpu.VMEM((tokens, features), F32),
                pltpu.VMEM((TICKS, tokens, features), BF16),
                pltpu.VMEM((TICKS, tokens, features), BF16),
                pltpu.VMEM((tokens, features), BF16),
                pltpu.VMEM((2 * tokens, features), BF16),
                pltpu.VMEM((2 * tokens, features), BF16),
                pltpu.VMEM((tokens, features), BF16),
                pltpu.VMEM((tokens, features), BF16),
                pltpu.VMEM((tokens, hidden_width), BF16),
                pltpu.VMEM((2, tokens // 2, tokens), F32),
                pltpu.VMEM((links, tokens, features), BF16),
                pltpu.VMEM((links, tokens, features), BF16),
                pltpu.SemaphoreType.DMA((4,)),
                pltpu.SemaphoreType.DMA((TICKS, 2)),
                pltpu.SemaphoreType.DMA((TICKS, 2)),
                pltpu.SemaphoreType.DMA((links, parts)),
                pltpu.SemaphoreType.DMA((links, parts)),
            ],
            compiler_params=pltpu.CompilerParams(
                collective_id=0, has_side_effects=True, vmem_limit_bytes=60 * 1024 * 1024
            ),
        )(
            member_codes,
            window_offset,
            logit_scale[0],
            member_slabs.reshape(tokens, features),
            member_table,
            land_sea.astype(F32).reshape(tokens, 1),
            land_embed,
            attention_gain,
            feed_gain,
            position_kernel[0],
            project_in[0],
            project_out[0],
            expand_weight[0],
            reduce_weight[0],
        )
        return updated.reshape(member_slabs.shape)

    placed = (
        P(("groups", "section"), "lat", None, None),
        P(None, "groups"),
        P(),
        P("lat", None),
        P("section", None),
        P("section", None),
        P("section", None, None),
        P("section", None),
        P("section", None, None, None),
        P("section", None, None),
        P("section", None),
        P("section", None, None),
        P("section", None, None),
        P("section"),
    )
    return jax.shard_map(
        body,
        mesh=mesh,
        in_specs=placed,
        out_specs=P(("groups", "section"), "lat", None, None),
        check_vma=False,
    )
```

```python
import functools
import math

import jax
import jax.numpy as jnp
from jax import lax
from jax.experimental import pallas as pl
from jax.experimental.pallas import tpu as pltpu
from jax.sharding import PartitionSpec as P

WIN_LAT = 4
WIN_LON = 32
TICKS = 2
EPSILON = 1e-06

F32 = jnp.float32
BF16 = jnp.bfloat16
LANES = 128
COLS = 256
MESH = pl.DeviceIdType.MESH


def norm_scale(values, gain_row):
    mean_square = jnp.mean(values * values, axis=-1, keepdims=True)
    return values * lax.rsqrt(mean_square + EPSILON) * gain_row


def dot(left, right):
    return jnp.dot(left, right, preferred_element_type=F32)


def head_unit(values, head_width):
    groups = []
    for start in range(0, values.shape[1], LANES):
        part = values[:, start : start + LANES]
        lane = lax.broadcasted_iota(jnp.int32, part.shape, 1)
        square = part * part
        factor = None
        for low in range(0, LANES, head_width):
            inside = (lane >= low) & (lane < low + head_width)
            total = jnp.sum(jnp.where(inside, square, 0.0), axis=-1, keepdims=True)
            scale = lax.rsqrt(total + EPSILON)
            factor = scale if factor is None else jnp.where(inside, scale, factor)
        groups.append((part * factor).astype(BF16))
    return jnp.concatenate(groups, axis=1)


def split_index(index, length, count):
    whole = jnp.zeros_like(index)
    for step in range(1, count):
        whole = whole + (index >= step * length).astype(jnp.int32)
    return whole, index - whole * length


def kernel(
    sizes,
    codes,
    offsets,
    head_scale,
    slab,
    table,
    land,
    land_embed,
    attention_gain,
    feed_gain,
    position_kernel,
    in_hbm,
    out_hbm,
    up_hbm,
    down_hbm,
    result,
    w_in,
    w_out,
    w_up,
    w_down,
    stream,
    mixed,
    normed,
    halo,
    queries,
    keys,
    values,
    blended,
    normed_mix,
    hidden,
    window,
    land_column,
    ring_out,
    ring_in,
    weight_sem,
    halo_send,
    halo_recv,
    ring_send,
    ring_recv,
):
    section_count, band_count, lon_cells, head_width = sizes
    tokens, features = slab.shape
    band_rows = tokens // lon_cells
    half = tokens // 2
    per_group = LANES // head_width
    section = lax.axis_index("section")
    band = lax.axis_index("lat")
    following = lax.rem(section + 1, section_count)
    preceding = lax.rem(section + section_count - 1, section_count)
    has_low = band > 0
    has_high = band < band_count - 1
    shifted = lax.rem(section, 2)

    barrier = pltpu.get_barrier_semaphore()
    pl.semaphore_signal(barrier, inc=1, device_id={"section": following}, device_id_type=MESH)
    pl.semaphore_signal(barrier, inc=1, device_id={"section": preceding}, device_id_type=MESH)

    @pl.when(has_low)
    def _():
        pl.semaphore_signal(barrier, inc=1, device_id={"lat": band - 1}, device_id_type=MESH)

    @pl.when(has_high)
    def _():
        pl.semaphore_signal(barrier, inc=1, device_id={"lat": band + 1}, device_id_type=MESH)

    loads = [
        pltpu.make_async_copy(source, target, weight_sem.at[index])
        for index, (source, target) in enumerate(
            ((in_hbm, w_in), (out_hbm, w_out), (up_hbm, w_up), (down_hbm, w_down))
        )
    ]
    loads[0].start()

    square = (lon_cells, lon_cells)
    diagonal = lax.broadcasted_iota(jnp.int32, square, 0) == lax.broadcasted_iota(jnp.int32, square, 1)
    for row in range(band_rows):
        marks = jnp.broadcast_to(land[row : row + 1, :].astype(F32), square)
        land_column[row * lon_cells : (row + 1) * lon_cells, :] = jnp.sum(
            jnp.where(diagonal, marks, 0.0), axis=-1, keepdims=True
        )

    offset = offsets[0] * shifted
    key_starts = [half * (1 - shifted), half + half * shifted]
    for side in range(2):
        shape = (half, tokens)
        first_row = band * band_rows - band_rows // 2 + (
            (1 - shifted) * (band_rows // 2) if side == 0 else (1 + shifted) * (band_rows // 2)
        )
        _, query_lon = split_index(lax.broadcasted_iota(jnp.int32, shape, 0), lon_cells, band_rows)
        key_row, key_lon = split_index(lax.broadcasted_iota(jnp.int32, shape, 1), lon_cells, band_rows)
        tiles = []
        for lon in (query_lon, key_lon):
            moved = lon - offset
            moved = jnp.where(moved < 0, moved + lon_cells, moved)
            tiles.append(split_index(moved, WIN_LON, lon_cells // WIN_LON)[0])
        row = key_row + first_row
        inside = (tiles[0] == tiles[1]) & (row >= 0) & (row < band_rows * band_count)
        window[side] = jnp.where(inside, 1.0, 0.0)

    def project(source, target_rows, with_queries):
        def step(index, carry):
            start = index * COLS
            columns = pl.ds(start, COLS)
            rows = source[...]
            if with_queries:
                queries[:, columns] = head_unit(dot(rows, w_in[:, columns]), head_width)
            key = head_unit(
                dot(rows, w_in[:, pl.ds(features + start, COLS)]), head_width
            )
            value = dot(
                rows, w_in[:, pl.ds(2 * features + start, COLS)]
            ).astype(BF16)
            done = 0
            for first, count in target_rows:
                keys[first : first + count, columns] = key[done : done + count]
                values[first : first + count, columns] = value[done : done + count]
                done += count
            return carry

        for index in range(features // COLS):
            step(index, 0)

    def attend(index, carry):
        columns = pl.ds(index * LANES, LANES)
        lane = lax.broadcasted_iota(jnp.int32, (1, LANES), 1)
        own = [
            jnp.where((lane >= low) & (lane < low + head_width), 1.0, 0.0).astype(BF16)
            for low in range(0, LANES, head_width)
        ]
        taps = [
            [position_kernel[lat * 3 + lon, :, columns] for lon in range(3)]
            for lat in range(WIN_LAT + 1)
        ]
        for side in range(2):
            spots = []
            for row in range(side * band_rows // 2, (side + 1) * band_rows // 2):
                strips = [
                    values[(row + lat) * lon_cells : (row + lat + 1) * lon_cells, columns].astype(F32)
                    for lat in range(WIN_LAT + 1)
                ]
                parts = []
                for lon in range(3):
                    part = taps[0][lon] * strips[0]
                    for lat in range(1, WIN_LAT + 1):
                        part = part + taps[lat][lon] * strips[lat]
                    parts.append(part)
                spots.append(
                    parts[1]
                    + pltpu.roll(parts[0], 1, 0)
                    + pltpu.roll(parts[2], lon_cells - 1, 0)
                )
            total = jnp.concatenate(spots, axis=0)
            near = pl.ds(pl.multiple_of(key_starts[side], half), tokens)
            key = keys[near, columns]
            value = values[near, columns]
            query = queries[side * half : (side + 1) * half, columns]
            scores = lax.dot_general(
                jnp.concatenate([query * mark for mark in own], axis=0),
                key,
                (((1,), (1,)), ((), ())),
                preferred_element_type=F32,
            )
            weights = []
            for head in range(per_group):
                mine = scores[head * half : (head + 1) * half]
                raised = jnp.exp(mine * head_scale[index * per_group + head]) * window[side]
                inverse = 1.0 / jnp.sum(raised, axis=-1, keepdims=True)
                weights.append((raised * inverse).astype(BF16))
            found = dot(jnp.concatenate(weights, axis=0), value)
            attended = found[:half]
            for head in range(1, per_group):
                attended = jnp.where(
                    lane >= head * head_width, found[head * half : (head + 1) * half], attended
                )
            total = total + attended
            blended[side * half : (side + 1) * half, columns] = total.astype(BF16)
        return carry

    def expand(index, carry):
        columns = pl.ds(index * COLS, COLS)
        wide = dot(normed_mix[...], w_up[:, columns])
        hidden[:, columns] = (wide * 0.5 * (1.0 + lax.erf(wide * math.sqrt(0.5)))).astype(BF16)
        return carry

    def halo_copies(tick):
        up = pltpu.make_async_remote_copy(
            src_ref=normed.at[tick, pl.ds(half, half)],
            dst_ref=halo.at[tick, pl.ds(0, half)],
            send_sem=halo_send.at[tick, 0],
            recv_sem=halo_recv.at[tick, 0],
            device_id={"lat": jnp.minimum(band + 1, band_count - 1)},
            device_id_type=MESH,
        )
        down = pltpu.make_async_remote_copy(
            src_ref=normed.at[tick, pl.ds(0, half)],
            dst_ref=halo.at[tick, pl.ds(half, half)],
            send_sem=halo_send.at[tick, 1],
            recv_sem=halo_recv.at[tick, 1],
            device_id={"lat": jnp.maximum(band - 1, 0)},
            device_id_type=MESH,
        )
        return up, down

    def ring_copy(tick, part):
        columns = pl.ds(part * COLS, COLS)
        return pltpu.make_async_remote_copy(
            src_ref=ring_out.at[tick, :, columns],
            dst_ref=ring_in.at[tick, :, columns],
            send_sem=ring_send.at[tick, part],
            recv_sem=ring_recv.at[tick, part],
            device_id={"section": following},
            device_id_type=MESH,
        )

    parts = features // COLS
    for tick in range(TICKS):
        if tick:
            for part in range(parts):
                ring_copy(tick - 1, part).wait()
        member = lax.rem(section - tick + section_count * TICKS, section_count)
        code = codes[tick, member]
        table_row = lax.broadcasted_iota(jnp.int32, table.shape, 0)
        perturb = jnp.sum(jnp.where(table_row == code, table[...], 0.0), axis=0, keepdims=True)

        def enter(index, carry):
            rows = pl.ds(pl.multiple_of(index * lon_cells, lon_cells), lon_cells)
            current = slab[rows, :] if tick == 0 else ring_in[tick - 1, rows, :].astype(F32)
            current = current + perturb + land_column[rows, :] * land_embed[...]
            stream[rows, :] = current
            normed[tick, rows, :] = norm_scale(current, attention_gain[...]).astype(BF16)
            return carry

        lax.fori_loop(0, band_rows, enter, 0)

        if tick == 0:
            ends = (band == 0).astype(jnp.int32) + (band == band_count - 1).astype(jnp.int32)
            pl.semaphore_wait(barrier, 4 - ends)

        up, down = halo_copies(tick)

        @pl.when(has_high)
        def _():
            up.start()

        @pl.when(has_low)
        def _():
            down.start()

        @pl.when(jnp.logical_not(has_low))
        def _():
            halo[tick, 0:half, :] = jnp.zeros((half, features), BF16)

        @pl.when(jnp.logical_not(has_high))
        def _():
            halo[tick, half:tokens, :] = jnp.zeros((half, features), BF16)

        if tick == 0:
            loads[0].wait()
            for load in loads[1:]:
                load.start()
        project(normed.at[tick], ((half, tokens),), True)

        @pl.when(has_high)
        def _():
            up.wait_send()
            down.wait_recv()

        @pl.when(has_low)
        def _():
            down.wait_send()
            up.wait_recv()

        project(halo.at[tick], ((0, half), (half + tokens, half)), False)
        for index in range(features // LANES):
            attend(index, 0)

        if tick == 0:
            loads[1].wait()
        for part in range(parts):
            columns = slice(part * COLS, (part + 1) * COLS)
            mixed[:, columns] = stream[:, columns] + dot(blended[...], w_out[:, columns])

        def middle(index, carry):
            rows = pl.ds(pl.multiple_of(index * lon_cells, lon_cells), lon_cells)
            normed_mix[rows, :] = norm_scale(mixed[rows, :], feed_gain[...]).astype(BF16)
            return carry

        lax.fori_loop(0, band_rows, middle, 0)
        if tick == 0:
            loads[2].wait()
        for index in range(w_up.shape[1] // COLS):
            expand(index, 0)
        if tick == 0:
            loads[3].wait()
        for part in range(parts):
            columns = slice(part * COLS, (part + 1) * COLS)
            finished = mixed[:, columns] + dot(hidden[...], w_down[:, columns])
            if tick + 1 < TICKS:
                ring_out[tick, :, columns] = finished.astype(BF16)
                ring_copy(tick, part).start()
            else:
                result[:, columns] = finished


def solution(mesh):
    section_count = mesh.shape["section"]
    band_count = mesh.shape["lat"]

    def body(
        member_slabs,
        member_codes,
        member_table,
        land_sea,
        land_embed,
        attention_gain,
        project_in,
        logit_scale,
        position_kernel,
        project_out,
        feed_gain,
        expand_weight,
        reduce_weight,
        window_offset,
    ):
        _, band_rows, lon_cells, features = member_slabs.shape
        assert band_rows == WIN_LAT
        tokens = band_rows * lon_cells
        hidden_width = expand_weight.shape[2]
        head_width = features // logit_scale.shape[1]
        parts = features // COLS
        links = max(TICKS - 1, 1)
        smem = pl.BlockSpec(memory_space=pltpu.SMEM)
        vmem = pl.BlockSpec(memory_space=pltpu.VMEM)
        hbm = pl.BlockSpec(memory_space=pl.ANY)
        updated = pl.pallas_call(
            functools.partial(kernel, (section_count, band_count, lon_cells, head_width)),
            out_shape=jax.ShapeDtypeStruct((tokens, features), F32),
            in_specs=[smem] * 3 + [vmem] * 7 + [hbm] * 4,
            out_specs=vmem,
            scratch_shapes=[
                pltpu.VMEM((features, 3 * features), BF16),
                pltpu.VMEM((features, features), BF16),
                pltpu.VMEM((features, hidden_width), BF16),
                pltpu.VMEM((hidden_width, features), BF16),
                pltpu.VMEM((tokens, features), F32),
                pltpu.VMEM((tokens, features), F32),
                pltpu.VMEM((TICKS, tokens, features), BF16),
                pltpu.VMEM((TICKS, tokens, features), BF16),
                pltpu.VMEM((tokens, features), BF16),
                pltpu.VMEM((2 * tokens, features), BF16),
                pltpu.VMEM((2 * tokens, features), BF16),
                pltpu.VMEM((tokens, features), BF16),
                pltpu.VMEM((tokens, features), BF16),
                pltpu.VMEM((tokens, hidden_width), BF16),
                pltpu.VMEM((2, tokens // 2, tokens), F32),
                pltpu.VMEM((tokens, 1), F32),
                pltpu.VMEM((links, tokens, features), BF16),
                pltpu.VMEM((links, tokens, features), BF16),
                pltpu.SemaphoreType.DMA((4,)),
                pltpu.SemaphoreType.DMA((TICKS, 2)),
                pltpu.SemaphoreType.DMA((TICKS, 2)),
                pltpu.SemaphoreType.DMA((links, parts)),
                pltpu.SemaphoreType.DMA((links, parts)),
            ],
            compiler_params=pltpu.CompilerParams(
                collective_id=0, has_side_effects=True, vmem_limit_bytes=60 * 1024 * 1024
            ),
        )(
            member_codes,
            window_offset,
            logit_scale[0],
            member_slabs.reshape(tokens, features),
            member_table,
            land_sea,
            land_embed,
            attention_gain,
            feed_gain,
            position_kernel.reshape(-1, 1, features),
            project_in[0],
            project_out[0],
            expand_weight[0],
            reduce_weight[0],
        )
        return updated.reshape(member_slabs.shape)

    placed = (
        P(("groups", "section"), "lat", None, None),
        P(None, "groups"),
        P(),
        P("lat", None),
        P("section", None),
        P("section", None),
        P("section", None, None),
        P("section", None),
        P("section", None, None, None),
        P("section", None, None),
        P("section", None),
        P("section", None, None),
        P("section", None, None),
        P("section"),
    )
    return jax.shard_map(
        body,
        mesh=mesh,
        in_specs=placed,
        out_specs=P(("groups", "section"), "lat", None, None),
        check_vma=False,
    )
```

```python
import functools
import math

import jax
import jax.numpy as jnp
from jax import lax
from jax.experimental import pallas as pl
from jax.experimental.pallas import tpu as pltpu
from jax.sharding import PartitionSpec as P

WIN_LAT = 4
WIN_LON = 32
TICKS = 2
EPSILON = 1e-06

F32 = jnp.float32
BF16 = jnp.bfloat16
LANES = 128
COLS = 256
MESH = pl.DeviceIdType.MESH


def norm_scale(values, gain_row):
    mean_square = jnp.mean(values * values, axis=-1, keepdims=True)
    return values * lax.rsqrt(mean_square + EPSILON) * gain_row


def dot(left, right):
    return jnp.dot(left, right, preferred_element_type=F32)


def head_unit(values, head_width):
    groups = []
    for start in range(0, values.shape[1], LANES):
        part = values[:, start : start + LANES]
        lane = lax.broadcasted_iota(jnp.int32, part.shape, 1)
        square = part * part
        factor = None
        for low in range(0, LANES, head_width):
            inside = (lane >= low) & (lane < low + head_width)
            total = jnp.sum(jnp.where(inside, square, 0.0), axis=-1, keepdims=True)
            scale = lax.rsqrt(total + EPSILON)
            factor = scale if factor is None else jnp.where(inside, scale, factor)
        groups.append((part * factor).astype(BF16))
    return jnp.concatenate(groups, axis=1)


def split_index(index, length, count):
    whole = jnp.zeros_like(index)
    for step in range(1, count):
        whole = whole + (index >= step * length).astype(jnp.int32)
    return whole, index - whole * length


def kernel(
    sizes,
    codes,
    offsets,
    head_scale,
    slab,
    table,
    land,
    land_embed,
    attention_gain,
    feed_gain,
    position_kernel,
    in_hbm,
    out_hbm,
    up_hbm,
    down_hbm,
    result,
    w_in,
    w_out,
    w_up,
    w_down,
    stream,
    mixed,
    normed,
    halo,
    queries,
    keys,
    values,
    blended,
    normed_mix,
    hidden,
    window,
    land_column,
    ring_out,
    ring_in,
    weight_sem,
    halo_send,
    halo_recv,
    ring_send,
    ring_recv,
):
    section_count, band_count, lon_cells, head_width = sizes
    tokens, features = slab.shape
    band_rows = tokens // lon_cells
    half = tokens // 2
    per_group = LANES // head_width
    section = lax.axis_index("section")
    band = lax.axis_index("lat")
    following = lax.rem(section + 1, section_count)
    preceding = lax.rem(section + section_count - 1, section_count)
    has_low = band > 0
    has_high = band < band_count - 1
    shifted = lax.rem(section, 2)

    barrier = pltpu.get_barrier_semaphore()
    pl.semaphore_signal(barrier, inc=1, device_id={"section": following}, device_id_type=MESH)
    pl.semaphore_signal(barrier, inc=1, device_id={"section": preceding}, device_id_type=MESH)

    @pl.when(has_low)
    def _():
        pl.semaphore_signal(barrier, inc=1, device_id={"lat": band - 1}, device_id_type=MESH)

    @pl.when(has_high)
    def _():
        pl.semaphore_signal(barrier, inc=1, device_id={"lat": band + 1}, device_id_type=MESH)

    loads = [
        pltpu.make_async_copy(source, target, weight_sem.at[index])
        for index, (source, target) in enumerate(
            ((out_hbm, w_out), (up_hbm, w_up), (down_hbm, w_down))
        )
    ]
    in_loads = []
    for start in range(0, features, COLS):
        for base in range(0, 3 * features, features):
            columns = pl.ds(base + start, COLS)
            in_loads.append(
                pltpu.make_async_copy(
                    in_hbm.at[:, columns], w_in.at[:, columns], weight_sem.at[3 + len(in_loads)]
                )
            )
    for load in in_loads:
        load.start()

    square = (lon_cells, lon_cells)
    diagonal = lax.broadcasted_iota(jnp.int32, square, 0) == lax.broadcasted_iota(jnp.int32, square, 1)
    for row in range(band_rows):
        marks = jnp.broadcast_to(land[row : row + 1, :].astype(F32), square)
        land_column[row * lon_cells : (row + 1) * lon_cells, :] = jnp.sum(
            jnp.where(diagonal, marks, 0.0), axis=-1, keepdims=True
        )

    offset = offsets[0] * shifted
    key_starts = [half * (1 - shifted), half + half * shifted]
    for side in range(2):
        shape = (half, tokens)
        first_row = band * band_rows - band_rows // 2 + (
            (1 - shifted) * (band_rows // 2) if side == 0 else (1 + shifted) * (band_rows // 2)
        )
        _, query_lon = split_index(lax.broadcasted_iota(jnp.int32, shape, 0), lon_cells, band_rows)
        key_row, key_lon = split_index(lax.broadcasted_iota(jnp.int32, shape, 1), lon_cells, band_rows)
        tiles = []
        for lon in (query_lon, key_lon):
            moved = lon - offset
            moved = jnp.where(moved < 0, moved + lon_cells, moved)
            tiles.append(split_index(moved, WIN_LON, lon_cells // WIN_LON)[0])
        row = key_row + first_row
        inside = (tiles[0] == tiles[1]) & (row >= 0) & (row < band_rows * band_count)
        window[side] = jnp.where(inside, 1.0, 0.0)

    def project(source, target_rows, with_queries, loading):
        def step(index, carry):
            if loading:
                for load in in_loads[3 * index : 3 * index + 3]:
                    load.wait()
            start = index * COLS
            columns = pl.ds(start, COLS)
            rows = source[...]
            if with_queries:
                queries[:, columns] = head_unit(dot(rows, w_in[:, columns]), head_width)
            key = head_unit(
                dot(rows, w_in[:, pl.ds(features + start, COLS)]), head_width
            )
            value = dot(
                rows, w_in[:, pl.ds(2 * features + start, COLS)]
            ).astype(BF16)
            done = 0
            for first, count in target_rows:
                keys[first : first + count, columns] = key[done : done + count]
                values[first : first + count, columns] = value[done : done + count]
                done += count
            return carry

        for index in range(features // COLS):
            step(index, 0)

    def attend(index, carry):
        columns = pl.ds(index * LANES, LANES)
        lane = lax.broadcasted_iota(jnp.int32, (1, LANES), 1)
        own = [
            jnp.where((lane >= low) & (lane < low + head_width), 1.0, 0.0).astype(BF16)
            for low in range(0, LANES, head_width)
        ]
        taps = [
            [position_kernel[lat * 3 + lon, :, columns] for lon in range(3)]
            for lat in range(WIN_LAT + 1)
        ]
        for side in range(2):
            spots = []
            for row in range(side * band_rows // 2, (side + 1) * band_rows // 2):
                strips = [
                    values[(row + lat) * lon_cells : (row + lat + 1) * lon_cells, columns].astype(F32)
                    for lat in range(WIN_LAT + 1)
                ]
                parts = []
                for lon in range(3):
                    part = taps[0][lon] * strips[0]
                    for lat in range(1, WIN_LAT + 1):
                        part = part + taps[lat][lon] * strips[lat]
                    parts.append(part)
                spots.append(
                    parts[1]
                    + pltpu.roll(parts[0], 1, 0)
                    + pltpu.roll(parts[2], lon_cells - 1, 0)
                )
            total = jnp.concatenate(spots, axis=0)
            near = pl.ds(pl.multiple_of(key_starts[side], half), tokens)
            key = keys[near, columns]
            value = values[near, columns]
            query = queries[side * half : (side + 1) * half, columns]
            scores = lax.dot_general(
                jnp.concatenate([query * mark for mark in own], axis=0),
                key,
                (((1,), (1,)), ((), ())),
                preferred_element_type=F32,
            )
            weights = []
            for head in range(per_group):
                mine = scores[head * half : (head + 1) * half]
                raised = jnp.exp(mine * head_scale[index * per_group + head]) * window[side]
                inverse = 1.0 / jnp.sum(raised, axis=-1, keepdims=True)
                weights.append((raised * inverse).astype(BF16))
            found = dot(jnp.concatenate(weights, axis=0), value)
            attended = found[:half]
            for head in range(1, per_group):
                attended = jnp.where(
                    lane >= head * head_width, found[head * half : (head + 1) * half], attended
                )
            total = total + attended
            blended[side * half : (side + 1) * half, columns] = total.astype(BF16)
        return carry

    def expand(index, carry):
        columns = pl.ds(index * COLS, COLS)
        wide = dot(normed_mix[...], w_up[:, columns])
        hidden[:, columns] = (wide * 0.5 * (1.0 + lax.erf(wide * math.sqrt(0.5)))).astype(BF16)
        return carry

    def halo_copies(tick):
        up = pltpu.make_async_remote_copy(
            src_ref=normed.at[tick, pl.ds(half, half)],
            dst_ref=halo.at[tick, pl.ds(0, half)],
            send_sem=halo_send.at[tick, 0],
            recv_sem=halo_recv.at[tick, 0],
            device_id={"lat": jnp.minimum(band + 1, band_count - 1)},
            device_id_type=MESH,
        )
        down = pltpu.make_async_remote_copy(
            src_ref=normed.at[tick, pl.ds(0, half)],
            dst_ref=halo.at[tick, pl.ds(half, half)],
            send_sem=halo_send.at[tick, 1],
            recv_sem=halo_recv.at[tick, 1],
            device_id={"lat": jnp.maximum(band - 1, 0)},
            device_id_type=MESH,
        )
        return up, down

    def ring_copy(tick, part):
        columns = pl.ds(part * COLS, COLS)
        return pltpu.make_async_remote_copy(
            src_ref=ring_out.at[tick, :, columns],
            dst_ref=ring_in.at[tick, :, columns],
            send_sem=ring_send.at[tick, part],
            recv_sem=ring_recv.at[tick, part],
            device_id={"section": following},
            device_id_type=MESH,
        )

    parts = features // COLS
    for tick in range(TICKS):
        if tick:
            for part in range(parts):
                ring_copy(tick - 1, part).wait()
        member = lax.rem(section - tick + section_count * TICKS, section_count)
        code = codes[tick, member]
        table_row = lax.broadcasted_iota(jnp.int32, table.shape, 0)
        perturb = jnp.sum(jnp.where(table_row == code, table[...], 0.0), axis=0, keepdims=True)

        def enter(index, carry):
            rows = pl.ds(index * lon_cells, lon_cells)
            current = slab[rows, :] if tick == 0 else ring_in[tick - 1, rows, :].astype(F32)
            current = current + perturb + land_column[rows, :] * land_embed[...]
            stream[rows, :] = current
            normed[tick, rows, :] = norm_scale(current, attention_gain[...]).astype(BF16)
            return carry

        for index in range(band_rows):
            enter(index, 0)

        if tick == 0:
            ends = (band == 0).astype(jnp.int32) + (band == band_count - 1).astype(jnp.int32)
            pl.semaphore_wait(barrier, 4 - ends)

        up, down = halo_copies(tick)

        @pl.when(has_high)
        def _():
            up.start()

        @pl.when(has_low)
        def _():
            down.start()

        @pl.when(jnp.logical_not(has_low))
        def _():
            halo[tick, 0:half, :] = jnp.zeros((half, features), BF16)

        @pl.when(jnp.logical_not(has_high))
        def _():
            halo[tick, half:tokens, :] = jnp.zeros((half, features), BF16)

        if tick == 0:
            for load in loads:
                load.start()
        project(normed.at[tick], ((half, tokens),), True, tick == 0)

        @pl.when(has_high)
        def _():
            up.wait_send()
            down.wait_recv()

        @pl.when(has_low)
        def _():
            down.wait_send()
            up.wait_recv()

        project(halo.at[tick], ((0, half), (half + tokens, half)), False, False)
        for index in range(features // LANES):
            attend(index, 0)

        if tick == 0:
            loads[0].wait()
        for part in range(parts):
            columns = slice(part * COLS, (part + 1) * COLS)
            mixed[:, columns] = stream[:, columns] + dot(blended[...], w_out[:, columns])

        def middle(index, carry):
            rows = pl.ds(index * lon_cells, lon_cells)
            normed_mix[rows, :] = norm_scale(mixed[rows, :], feed_gain[...]).astype(BF16)
            return carry

        for index in range(band_rows):
            middle(index, 0)
        if tick == 0:
            loads[1].wait()
        for index in range(w_up.shape[1] // COLS):
            expand(index, 0)
        if tick == 0:
            loads[2].wait()
        for part in range(parts):
            columns = slice(part * COLS, (part + 1) * COLS)
            finished = mixed[:, columns] + dot(hidden[...], w_down[:, columns])
            if tick + 1 < TICKS:
                ring_out[tick, :, columns] = finished.astype(BF16)
                ring_copy(tick, part).start()
            else:
                result[:, columns] = finished


def solution(mesh):
    section_count = mesh.shape["section"]
    band_count = mesh.shape["lat"]

    def body(
        member_slabs,
        member_codes,
        member_table,
        land_sea,
        land_embed,
        attention_gain,
        project_in,
        logit_scale,
        position_kernel,
        project_out,
        feed_gain,
        expand_weight,
        reduce_weight,
        window_offset,
    ):
        _, band_rows, lon_cells, features = member_slabs.shape
        assert band_rows == WIN_LAT
        tokens = band_rows * lon_cells
        hidden_width = expand_weight.shape[2]
        head_width = features // logit_scale.shape[1]
        parts = features // COLS
        links = max(TICKS - 1, 1)
        smem = pl.BlockSpec(memory_space=pltpu.SMEM)
        vmem = pl.BlockSpec(memory_space=pltpu.VMEM)
        hbm = pl.BlockSpec(memory_space=pl.ANY)
        updated = pl.pallas_call(
            functools.partial(kernel, (section_count, band_count, lon_cells, head_width)),
            out_shape=jax.ShapeDtypeStruct((tokens, features), F32),
            in_specs=[smem] * 3 + [vmem] * 7 + [hbm] * 4,
            out_specs=vmem,
            scratch_shapes=[
                pltpu.VMEM((features, 3 * features), BF16),
                pltpu.VMEM((features, features), BF16),
                pltpu.VMEM((features, hidden_width), BF16),
                pltpu.VMEM((hidden_width, features), BF16),
                pltpu.VMEM((tokens, features), F32),
                pltpu.VMEM((tokens, features), F32),
                pltpu.VMEM((TICKS, tokens, features), BF16),
                pltpu.VMEM((TICKS, tokens, features), BF16),
                pltpu.VMEM((tokens, features), BF16),
                pltpu.VMEM((2 * tokens, features), BF16),
                pltpu.VMEM((2 * tokens, features), BF16),
                pltpu.VMEM((tokens, features), BF16),
                pltpu.VMEM((tokens, features), BF16),
                pltpu.VMEM((tokens, hidden_width), BF16),
                pltpu.VMEM((2, tokens // 2, tokens), F32),
                pltpu.VMEM((tokens, 1), F32),
                pltpu.VMEM((links, tokens, features), BF16),
                pltpu.VMEM((links, tokens, features), BF16),
                pltpu.SemaphoreType.DMA((3 + 3 * parts,)),
                pltpu.SemaphoreType.DMA((TICKS, 2)),
                pltpu.SemaphoreType.DMA((TICKS, 2)),
                pltpu.SemaphoreType.DMA((links, parts)),
                pltpu.SemaphoreType.DMA((links, parts)),
            ],
            compiler_params=pltpu.CompilerParams(
                collective_id=0, has_side_effects=True, vmem_limit_bytes=60 * 1024 * 1024
            ),
        )(
            member_codes,
            window_offset,
            logit_scale[0],
            member_slabs.reshape(tokens, features),
            member_table,
            land_sea,
            land_embed,
            attention_gain,
            feed_gain,
            position_kernel.reshape(-1, 1, features),
            project_in[0],
            project_out[0],
            expand_weight[0],
            reduce_weight[0],
        )
        return updated.reshape(member_slabs.shape)

    placed = (
        P(("groups", "section"), "lat", None, None),
        P(None, "groups"),
        P(),
        P("lat", None),
        P("section", None),
        P("section", None),
        P("section", None, None),
        P("section", None),
        P("section", None, None, None),
        P("section", None, None),
        P("section", None),
        P("section", None, None),
        P("section", None, None),
        P("section"),
    )
    return jax.shard_map(
        body,
        mesh=mesh,
        in_specs=placed,
        out_specs=P(("groups", "section"), "lat", None, None),
        check_vma=False,
    )
```
